32 devices in a mesh: chan: 4 (over y, x), hid: 8 (over z, core).
Axes of the slice: x: 2, y: 2, z: 4, core: 2. Of those that a mesh axis runs over, the one named last changes fastest.
Arguments:
- pixels: bfloat16 [384, 256, 256], P('chan'), may hold values from -6 to 6
- patch_weight: bfloat16 [384, 256, 6144], P('chan', None, 'hid'), may hold values from -0.375 to 0.375
- channel_embed: bfloat16 [384, 6144], P('chan', 'hid'), may hold values from -3 to 3
- pool_query: bfloat16 [48, 6144], P('chan', 'hid'), may hold values from -2.5 to 2.5
- group_mix: bfloat16 [48, 6144], P('chan', 'hid'), may hold values from -3.2 to 3.2
- assign: int32 [384], P('chan'), may hold values from 0 to 47, as said below
- ln_gain: float32 [6144], P('chan'), may hold values from 0.1 to 1.9
- w_qkv: bfloat16 [6144, 3, 6144], P('chan', None, 'hid'), may hold values from -0.078125 to 0.078125
- w_up: bfloat16 [6144, 24576], P('chan', 'hid'), may hold values from -0.078125 to 0.078125
- b_up: float32 [24576], P('hid'), may hold values from -3 to 3
- w_out: bfloat16 [6144, 6144], P('hid', 'chan'), may hold values from -0.078125 to 0.078125
- w_down: bfloat16 [24576, 6144], P('hid', 'chan'), may hold values from -0.0390625 to 0.0390625
Outputs:
- block_out: bfloat16 [256, 6144], P(None, 'chan')
The draws below stay inside these ranges and needn't reach their ends.
Inputs may be any that keep to these rules, and one draw needn't show every extreme that they name: Channel c belongs to group assign[c]; every group holds exactly 8 channels, and group k's channels all lie among the 96 consecutive channels beginning at channel (k // 12) * 96.
All inputs are finite; a program needn't handle non-finite values.
Results may differ from the reference program's by a relative error of at most 0.02.
Values may be sent and summed in bfloat16 or wider, within the bound.
A program may use at most 320 MiB of HBM per device.

```python
import math
import jax
import jax.numpy as jnp
from jax import lax

HS = 128
HEADS = 48
FF = 24576
C = 384
G = 48
P2 = 256
PATCHES = 256
IMAGES = 1
D = 6144
TOKENS = 256
CH_DEV = 96
G_DEV = 12


def draw_assign(key, part):
    blocks = C // CH_DEV
    raw_keys = jax.random.randint(key, (C,), 0, 1 << 20, dtype=jnp.int32) * C + jnp.arange(C, dtype=jnp.int32)
    row_keys = raw_keys.reshape(blocks, CH_DEV)
    rankings = jnp.argsort(jnp.argsort(row_keys, axis=1), axis=1).astype(jnp.int32)
    groups = jnp.arange(blocks, dtype=jnp.int32)[:, None] * G_DEV + rankings // (C // G)
    return groups.reshape(C).astype(jnp.int32)


def draw_group_mix(key, part):
    columns = jnp.arange(D, dtype=jnp.float32) / D
    base = jnp.clip(jax.random.normal(key, (G, D), jnp.float32), -4.0, 4.0)
    ramp = 0.08 * jnp.exp(math.log(10.0) * columns)
    return (base * ramp[None, :]).astype(jnp.bfloat16)


def shard_levels(stream_key, extent, shards, low, top_value):
    def one(dim, parts):
        steps = jax.random.uniform(jax.random.fold_in(jax.random.fold_in(stream_key, 6), dim), (parts,), jnp.float32, low / len(shards), top_value / len(shards))
        return jnp.repeat(jnp.exp(steps), extent[dim] // parts).reshape((-1,) + (1,) * (len(extent) - dim - 1))

    gain = one(*shards[0])
    for cut in shards[1:]:
        gain = gain * one(*cut)
    return gain


def scatter_about(key, shape, spread, bound, cuts=(), held_as=jnp.bfloat16):
    values = jax.random.normal(key, shape, jnp.float32) * spread
    if len(cuts) > 0:
        values = shard_levels(key, shape, cuts, -0.22, 0.18) * values
    return jnp.clip(values, min=-bound, max=bound).astype(held_as)


def setup_inputs(seed: int = 0) -> dict:
    seeds = jax.random.split(jax.random.key(seed), 13)
    pixels = scatter_about(seeds[0], (C, TOKENS, P2), 1.0, 6.0, ((0, 4),))
    patch_weight = scatter_about(seeds[1], (C, P2, D), P2 ** -0.5, 0.375, ((0, 4), (2, 8)))
    channel_embed = scatter_about(seeds[2], (C, D), 0.5, 3.0, ((0, 4), (1, 8)))
    pool_query = scatter_about(seeds[3], (G, D), 1.0, 2.5, ((0, 4), (1, 8)))
    group_mix = draw_group_mix(jax.random.fold_in(seeds[12], 71), 0)
    assign = draw_assign(jax.random.fold_in(seeds[12], 71), 0)
    ln_gain = jnp.clip(1.0 + 0.18 * jax.random.normal(seeds[6], (D,), jnp.float32), 0.1, 1.9)
    w_qkv = scatter_about(seeds[7], (D, 3, D), D ** -0.5, 0.078125, ((0, 4), (2, 8)))
    w_up = scatter_about(seeds[8], (D, FF), D ** -0.5, 0.078125, ((0, 4), (1, 8)))
    b_up = scatter_about(seeds[9], (FF,), 0.5, 3.0, ((0, 8),), jnp.float32)
    w_out = scatter_about(seeds[10], (D, D), D ** -0.5, 0.078125, ((0, 8), (1, 4)))
    w_down = scatter_about(seeds[11], (FF, D), FF ** -0.5, 0.0390625, ((0, 8), (1, 4)))
    return {"pixels": pixels, "patch_weight": patch_weight, "channel_embed": channel_embed, "pool_query": pool_query, "group_mix": group_mix, "assign": assign, "ln_gain": ln_gain, "w_qkv": w_qkv, "w_up": w_up, "b_up": b_up, "w_out": w_out, "w_down": w_down}


epsilon = 1e-06

def head_norm(values):
    return values * lax.rsqrt(lax.optimization_barrier(jnp.mean(values * values, axis=-1, keepdims=True)) + epsilon)

def reference(pixels, patch_weight, channel_embed, pool_query, group_mix, assign, ln_gain, w_qkv, w_up, b_up, w_out, w_down):
    group_size = C // G
    ordering = jnp.argsort(assign, stable=True).astype(jnp.int32).reshape(G, group_size)

    def add_group(carry, group_idx):
        members = ordering[group_idx]
        patches = pixels[members].astype(jnp.float32)
        weights = patch_weight[members].astype(jnp.float32)
        embedded = jnp.einsum('ctp,cpd->ctd', patches, weights, precision=lax.Precision.HIGHEST)
        embedded = embedded + channel_embed[members].astype(jnp.float32)[:, None, :]
        features = jax.nn.gelu(embedded, approximate=False)
        split = features.reshape(group_size, TOKENS, HEADS, HS)
        normed = head_norm(split)
        query = pool_query[group_idx].astype(jnp.float32).reshape(HEADS, HS)
        score = jnp.einsum('cthe,he->cth', normed, query, precision=lax.Precision.HIGHEST) / math.sqrt(HS)
        shift = jnp.sqrt(lax.optimization_barrier(jnp.sum(query * query, axis=-1)))
        weight = jnp.exp(score - shift)
        numer = lax.optimization_barrier(jnp.sum(weight[..., None] * split, axis=0))
        denom = lax.optimization_barrier(jnp.sum(weight, axis=0))
        pooled = (numer / denom[..., None]).reshape(TOKENS, D)
        return (carry + pooled * group_mix[group_idx].astype(jnp.float32), None)
    result = lax.scan(add_group, jnp.zeros((TOKENS, D), jnp.float32), jnp.arange(G, dtype=jnp.int32))
    layer_input = result[0].astype(jnp.bfloat16)
    wide = layer_input.astype(jnp.float32)
    row_mean = lax.optimization_barrier(jnp.sum(wide, axis=1)) / D
    row_var = lax.optimization_barrier(jnp.sum(wide * wide, axis=1)) / D - row_mean * row_mean
    normed_input = ((wide - row_mean[:, None]) * lax.rsqrt(row_var + epsilon)[:, None] * ln_gain).astype(jnp.bfloat16)
    qkv_sum = jnp.dot(normed_input, w_qkv.reshape(D, 3 * D), preferred_element_type=jnp.float32)
    up_sum = jnp.dot(normed_input, w_up, preferred_element_type=jnp.float32) + b_up
    heads = qkv_sum.reshape(IMAGES, PATCHES, 3, HEADS, HS)
    queries = head_norm(heads[:, :, 0]).astype(jnp.bfloat16)
    keys = head_norm(heads[:, :, 1]).astype(jnp.bfloat16)
    values = heads[:, :, 2].astype(jnp.bfloat16)
    scores = jnp.einsum('bqhe,bkhe->bhqk', queries.astype(jnp.float32), keys.astype(jnp.float32)) * (2.0 / math.sqrt(HS))
    expo = jnp.exp(scores)
    probs = (expo / lax.optimization_barrier(jnp.sum(expo, axis=-1, keepdims=True))).astype(jnp.bfloat16)
    attended = jnp.einsum('bhqk,bkhe->bqhe', probs.astype(jnp.float32), values.astype(jnp.float32))
    attended = attended.astype(jnp.bfloat16).reshape(TOKENS, D)
    hidden = jax.nn.gelu(up_sum, approximate=False).astype(jnp.bfloat16)
    mixed = jnp.dot(attended, w_out, preferred_element_type=jnp.float32) + jnp.dot(hidden, w_down, preferred_element_type=jnp.float32)
    return (wide + mixed).astype(jnp.bfloat16)
```

```python
import functools
import math

import jax
import jax.numpy as jnp
from jax import lax
from jax.experimental import pallas as pl
from jax.experimental.pallas import tpu as pltpu
from jax.sharding import PartitionSpec as P

HS = 128
PATCHES = 256
D = 6144


epsilon = 1e-06


def pool_kernel(size, order_ref, pix_ref, pw_ref, emb_ref, qb_ref, shift_ref, mix_ref, out_ref, feat, sq, numer, denom, acc):
    g = pl.program_id(0); j = pl.program_id(1)
    tok, width = acc.shape
    heads = width // HS
    lane = feat.shape[1]
    rows = lax.broadcasted_iota(jnp.int32, (width, HS), 0) // HS
    cols = lax.broadcasted_iota(jnp.int32, (width, HS), 1)
    pick = (rows == cols).astype(jnp.bfloat16)

    @pl.when((g == 0) & (j == 0))
    def _():
        acc[...] = jnp.zeros_like(acc)

    step = min(256, width)
    for n in range(width // step):
        cs = slice(n * step, (n + 1) * step)
        for r in range(0, tok, 64):
            e = jnp.dot(pix_ref[0, r:r+64], pw_ref[0, :, cs], preferred_element_type=jnp.float32)
            e = e + emb_ref[0, :, cs]
            f = (0.5 * e) * (1.0 + lax.erf(e * math.sqrt(0.5)))
            feat[r:r+64, cs] = f.astype(jnp.bfloat16)
            sq[r:r+64, cs] = (f * f).astype(jnp.bfloat16)
    dots = jnp.dot(feat[...], qb_ref[0], preferred_element_type=jnp.float32)
    total = jnp.dot(sq[...], pick, preferred_element_type=jnp.float32)
    score = dots * lax.rsqrt(total * (1.0 / HS) + epsilon) * (1.0 / math.sqrt(HS))
    weight = jnp.exp(score - shift_ref[0])
    @pl.when(j == 0)
    def _():
        denom[...] = weight
        for h in range(heads):
            hs = slice(h * HS, (h + 1) * HS)
            numer[:, hs] = weight[:, h:h+1] * feat[:, hs].astype(jnp.float32)
    @pl.when(j > 0)
    def _():
        denom[...] += weight
        for h in range(heads):
            hs = slice(h * HS, (h + 1) * HS)
            numer[:, hs] += weight[:, h:h+1] * feat[:, hs].astype(jnp.float32)
    @pl.when(j == size - 1)
    def _():
        inv = 1.0 / denom[...]
        for h in range(heads):
            hs = slice(h * HS, (h + 1) * HS)
            acc[:, hs] += numer[:, hs] * inv[:, h:h+1] * mix_ref[0, :, hs]
    @pl.when((g == pl.num_programs(0) - 1) & (j == size - 1))
    def _():
        out_ref[...] = acc[...].astype(jnp.bfloat16)

def pool(pixels, patch_weight, channel_embed, pool_query, group_mix, assign):
    chans, tok, p2 = pixels.shape
    width = patch_weight.shape[2]
    groups = pool_query.shape[0]
    size = chans // groups
    heads = width // HS
    idx = jnp.arange(chans, dtype=jnp.int32)
    key = assign * chans + idx
    rank = jnp.sum((key[None, :] < key[:, None]).astype(jnp.int32), axis=1)
    order = jnp.sum(jnp.where(rank[None, :] == idx[:, None], idx[None, :], 0), axis=1).astype(jnp.int32)
    q = pool_query.astype(jnp.float32)
    heads_of = jnp.arange(width, dtype=jnp.int32) // HS
    lanes = jnp.arange(HS, dtype=jnp.int32)
    qb = jnp.where(heads_of[None, :, None] == lanes[None, None, :], pool_query[:, :, None], jnp.bfloat16(0))
    sh = jnp.sqrt(jnp.sum((q * q).reshape(groups, heads, HS), axis=-1))
    sh = jnp.pad(sh, ((0, 0), (0, HS - heads))).reshape(groups, 1, HS)
    spec = pltpu.PrefetchScalarGridSpec(
        num_scalar_prefetch=1, grid=(groups, size),
        in_specs=[
            pl.BlockSpec((1, tok, p2), lambda g, j, o: (o[g * size + j], 0, 0)),
            pl.BlockSpec((1, p2, width), lambda g, j, o: (o[g * size + j], 0, 0)),
            pl.BlockSpec((1, 1, width), lambda g, j, o: (o[g * size + j], 0, 0)),
            pl.BlockSpec((1, width, HS), lambda g, j, o: (g, 0, 0)),
            pl.BlockSpec((1, 1, HS), lambda g, j, o: (g, 0, 0)),
            pl.BlockSpec((1, 1, width), lambda g, j, o: (g, 0, 0)),
        ],
        out_specs=pl.BlockSpec((tok, width), lambda g, j, o: (0, 0)),
        scratch_shapes=[
            pltpu.VMEM((tok, width), jnp.bfloat16), pltpu.VMEM((tok, width), jnp.bfloat16),
            pltpu.VMEM((tok, width), jnp.float32), pltpu.VMEM((tok, HS), jnp.float32),
            pltpu.VMEM((tok, width), jnp.float32)])
    return pl.pallas_call(
        functools.partial(pool_kernel, size), grid_spec=spec,
        out_shape=jax.ShapeDtypeStruct((tok, width), jnp.bfloat16),
        compiler_params=pltpu.CompilerParams(dimension_semantics=("arbitrary", "arbitrary"), vmem_limit_bytes=40 << 20),
        name="pool",
    )(order, pixels, patch_weight, channel_embed.astype(jnp.float32).reshape(chans, 1, width), qb, sh,
      group_mix.astype(jnp.float32).reshape(groups, 1, width))


def head_norm(values):
    return values * lax.rsqrt(jnp.mean(values * values, axis=-1, keepdims=True) + epsilon)


def finish_rows(qkv_rows, up_rows, b_up, heads_dev):
    rows = qkv_rows.shape[0]
    width = heads_dev * HS
    query_part = (
        head_norm(qkv_rows[:, 0].reshape(rows, heads_dev, HS))
        .astype(jnp.bfloat16)
        .reshape(rows, width)
    )
    key_part = (
        head_norm(qkv_rows[:, 1].reshape(rows, heads_dev, HS))
        .astype(jnp.bfloat16)
        .reshape(rows, width)
    )
    value_part = qkv_rows[:, 2].astype(jnp.bfloat16)
    hidden_part = jax.nn.gelu(up_rows + b_up, approximate=False).astype(jnp.bfloat16)
    return (query_part, key_part, value_part, hidden_part)


def on_device(
    pixels,
    patch_weight,
    channel_embed,
    pool_query,
    group_mix,
    assign,
    ln_gain,
    w_qkv,
    w_up,
    b_up,
    w_out,
    w_down,
):
    tok_count = pixels.shape[1]
    width_hid = patch_weight.shape[2]
    width_chan = ln_gain.shape[0]
    heads_dev = width_hid // HS
    partial_value = pool(pixels, patch_weight, channel_embed, pool_query, group_mix, assign)
    layer_sum = lax.psum(partial_value.astype(jnp.bfloat16), "chan")
    gathered = lax.all_gather(layer_sum, "hid", axis=1, tiled=True)
    wide = gathered.astype(jnp.float32)
    row_total = jnp.sum(wide, axis=1)
    row_square = jnp.sum(wide * wide, axis=1)
    mine = lax.dynamic_slice_in_dim(gathered, lax.axis_index("chan") * width_chan, width_chan, 1)
    row_mean = row_total / D
    row_var = row_square / D - row_mean * row_mean
    own_cols = mine.astype(jnp.float32)
    normed_input = (
        (own_cols - row_mean[:, None]) * lax.rsqrt(row_var + epsilon)[:, None] * ln_gain
    ).astype(jnp.bfloat16)
    qkv_part = jnp.einsum("td,dke->tke", normed_input, w_qkv, preferred_element_type=jnp.float32)
    up_part = jnp.dot(normed_input, w_up, preferred_element_type=jnp.float32)
    qkv_share, up_share = (
        lax.psum_scatter(
            qkv_part.astype(jnp.bfloat16), "chan", scatter_dimension=0, tiled=True
        ).astype(jnp.float32),
        lax.psum_scatter(
            up_part.astype(jnp.bfloat16), "chan", scatter_dimension=0, tiled=True
        ).astype(jnp.float32),
    )
    query_share, key_share, value_share, hidden_share = finish_rows(
        qkv_share, up_share, b_up, heads_dev
    )
    query_rows, key_rows, value_rows, hidden = (
        lax.all_gather(query_share, "chan", axis=0, tiled=True),
        lax.all_gather(key_share, "chan", axis=0, tiled=True),
        lax.all_gather(value_share, "chan", axis=0, tiled=True),
        lax.all_gather(hidden_share, "chan", axis=0, tiled=True),
    )
    images = tok_count // PATCHES
    queries = query_rows.reshape(images, PATCHES, heads_dev, HS)
    keys = key_rows.reshape(images, PATCHES, heads_dev, HS)
    values = value_rows.reshape(images, PATCHES, heads_dev, HS)
    scores = jnp.einsum("bqhe,bkhe->bhqk", queries, keys, preferred_element_type=jnp.float32) * (
        2.0 / math.sqrt(HS)
    )
    expo = jnp.exp(scores)
    probs = (expo / jnp.sum(expo, axis=-1, keepdims=True)).astype(jnp.bfloat16)
    attended = jnp.einsum("bhqk,bkhe->bqhe", probs, values, preferred_element_type=jnp.float32)
    attended = attended.astype(jnp.bfloat16).reshape(tok_count, width_hid)
    term = jnp.dot(attended, w_out, preferred_element_type=jnp.float32) + jnp.dot(
        hidden, w_down, preferred_element_type=jnp.float32
    )
    mixed = lax.psum(term.astype(jnp.bfloat16), "hid").astype(jnp.float32)
    return (own_cols + mixed).astype(jnp.bfloat16)


def solution(mesh):
    in_specs = (
        P("chan", None, None),
        P("chan", None, "hid"),
        P("chan", "hid"),
        P("chan", "hid"),
        P("chan", "hid"),
        P("chan"),
        P("chan"),
        P("chan", None, "hid"),
        P("chan", "hid"),
        P("hid"),
        P("hid", "chan"),
        P("hid", "chan"),
    )
    out_specs = P(None, "chan")
    return jax.shard_map(
        on_device, mesh=mesh, in_specs=in_specs, out_specs=out_specs, check_vma=False
    )
```

```python
import functools
import math

import jax
import jax.numpy as jnp
from jax import lax
from jax.experimental import pallas as pl
from jax.experimental.pallas import tpu as pltpu
from jax.sharding import PartitionSpec as P

HS = 128
PATCHES = 256


epsilon = 1e-06


def pool_kernel(size, order_ref, pix_ref, pw_ref, emb_ref, query_ref, shift_ref, mix_ref, out_ref, feat, sq, numer, denom, acc, pick, quer):
    g = pl.program_id(0); j = pl.program_id(1)
    tok, width = acc.shape
    heads = width // HS
    head = lax.broadcasted_iota(jnp.int32, (HS, width), 0)
    head_of = lax.broadcasted_iota(jnp.int32, (HS, width), 1) // HS

    @pl.when((g == 0) & (j == 0))
    def _():
        acc[...] = jnp.zeros_like(acc)
        pick[...] = jnp.where(head_of == head, 1.0, 0.0).astype(jnp.bfloat16)

    @pl.when(j == 0)
    def _():
        quer[...] = jnp.where(head_of == head, query_ref[0], 0.0).astype(jnp.bfloat16)

    across = (((1,), (1,)), ((), ()))
    step = min(256, width)
    for n in range(width // step):
        cs = slice(n * step, (n + 1) * step)
        for r in range(0, tok, 64):
            e = jnp.dot(pix_ref[0, r:r+64], pw_ref[0, :, cs], preferred_element_type=jnp.float32)
            e = e + emb_ref[0, :, cs]
            f = (0.5 * e) * (1.0 + lax.erf(e * math.sqrt(0.5)))
            feat[r:r+64, cs] = f.astype(jnp.bfloat16)
            sq[r:r+64, cs] = (f * f).astype(jnp.bfloat16)
    dots = lax.dot_general(feat[...], quer[...], across, preferred_element_type=jnp.float32)
    total = lax.dot_general(sq[...], pick[...], across, preferred_element_type=jnp.float32)
    score = dots * lax.rsqrt(total * (1.0 / HS) + epsilon) * (1.0 / math.sqrt(HS))
    weight = jnp.exp(score - shift_ref[0])
    @pl.when(j == 0)
    def _():
        denom[...] = weight
        for h in range(heads):
            hs = slice(h * HS, (h + 1) * HS)
            numer[:, hs] = weight[:, h:h+1] * feat[:, hs].astype(jnp.float32)
    @pl.when(j > 0)
    def _():
        denom[...] += weight
        for h in range(heads):
            hs = slice(h * HS, (h + 1) * HS)
            numer[:, hs] += weight[:, h:h+1] * feat[:, hs].astype(jnp.float32)
    @pl.when(j == size - 1)
    def _():
        inv = 1.0 / denom[...]
        for h in range(heads):
            hs = slice(h * HS, (h + 1) * HS)
            acc[:, hs] += numer[:, hs] * inv[:, h:h+1] * mix_ref[0, :, hs]
    @pl.when((g == pl.num_programs(0) - 1) & (j == size - 1))
    def _():
        out_ref[...] = acc[...].astype(jnp.bfloat16)

def pool(pixels, patch_weight, channel_embed, pool_query, group_mix, assign):
    chans, tok, p2 = pixels.shape
    width = patch_weight.shape[2]
    groups = pool_query.shape[0]
    size = chans // groups
    heads = width // HS
    idx = jnp.arange(chans, dtype=jnp.int32)
    key = assign * chans + idx
    rank = jnp.sum((key[None, :] < key[:, None]).astype(jnp.int32), axis=1)
    order = jnp.sum(jnp.where(rank[None, :] == idx[:, None], idx[None, :], 0), axis=1).astype(jnp.int32)
    q = pool_query.astype(jnp.float32)
    sh = jnp.sqrt(jnp.sum((q * q).reshape(groups, heads, HS), axis=-1))
    sh = jnp.pad(sh, ((0, 0), (0, HS - heads))).reshape(groups, 1, HS)
    spec = pltpu.PrefetchScalarGridSpec(
        num_scalar_prefetch=1, grid=(groups, size),
        in_specs=[
            pl.BlockSpec((1, tok, p2), lambda g, j, o: (o[g * size + j], 0, 0)),
            pl.BlockSpec((1, p2, width), lambda g, j, o: (o[g * size + j], 0, 0)),
            pl.BlockSpec((1, 1, width), lambda g, j, o: (o[g * size + j], 0, 0)),
            pl.BlockSpec((1, 1, width), lambda g, j, o: (g, 0, 0)),
            pl.BlockSpec((1, 1, HS), lambda g, j, o: (g, 0, 0)),
            pl.BlockSpec((1, 1, width), lambda g, j, o: (g, 0, 0)),
        ],
        out_specs=pl.BlockSpec((tok, width), lambda g, j, o: (0, 0)),
        scratch_shapes=[
            pltpu.VMEM((tok, width), jnp.bfloat16), pltpu.VMEM((tok, width), jnp.bfloat16),
            pltpu.VMEM((tok, width), jnp.float32), pltpu.VMEM((tok, HS), jnp.float32),
            pltpu.VMEM((tok, width), jnp.float32), pltpu.VMEM((HS, width), jnp.bfloat16), pltpu.VMEM((HS, width), jnp.bfloat16)])
    return pl.pallas_call(
        functools.partial(pool_kernel, size), grid_spec=spec,
        out_shape=jax.ShapeDtypeStruct((tok, width), jnp.bfloat16),
        compiler_params=pltpu.CompilerParams(dimension_semantics=("arbitrary", "arbitrary"), vmem_limit_bytes=40 << 20),
        name="pool",
    )(order, pixels, patch_weight, channel_embed.astype(jnp.float32).reshape(chans, 1, width), q.reshape(groups, 1, width), sh,
      group_mix.astype(jnp.float32).reshape(groups, 1, width))


def head_norm(values):
    return values * lax.rsqrt(jnp.mean(values * values, axis=-1, keepdims=True) + epsilon)


MESH = pl.DeviceIdType.MESH


def greet(peers):
    gate = pltpu.get_barrier_semaphore()
    for peer in peers:
        pl.semaphore_signal(gate, inc=1, device_id=peer, device_id_type=MESH)
    pl.semaphore_wait(gate, len(peers))


def send(src, dst, sems, slot, peer):
    copy = pltpu.make_async_remote_copy(
        src_ref=src, dst_ref=dst, send_sem=sems.at[0, slot], recv_sem=sems.at[1, slot],
        device_id=peer, device_id_type=MESH)
    copy.start()
    return copy


def places(chans, hids):
    a, b = lax.axis_index("chan"), lax.axis_index("hid")
    chips, chip, core = hids // 2, b // 2, b % 2
    rows = [{"chan": lax.rem(a + k, chans)} for k in range(1, chans)]
    far = [{"hid": lax.rem(chip + k, chips) * 2 + core} for k in range(1, chips)]
    return a, b, chips, chip, core, rows, far, {"hid": chip * 2 + (1 - core)}


def spread(src_of, slots, chips, chip, core, far, mate, away, near):
    sent = [send(src_of(chip * 2 + core), src_of(chip * 2 + core), away, k, peer) for k, peer in enumerate(far)]
    mine = src_of(chip * 2 + core)
    passed = [send(mine, mine, near, 0, mate)]
    for k in range(1, chips):
        sent[k - 1].wait_recv()
        piece = src_of(lax.rem(chip + chips - k, chips) * 2 + core)
        passed.append(send(piece, piece, near, k, mate))
    for copy in passed:
        copy.wait()
    for copy in sent:
        copy.wait_send()


def layer_kernel(chans, hids, part, gain, normed_ref, own_ref, parts, gath, stat, whole, stats, s1, s2, s3, s4, s5):
    a, b, chips, chip, core, rows, far, mate = places(chans, hids)
    greet(rows + far + [mate])
    width = part.shape[2]
    size = part.shape[1]
    copies = [send(part.at[lax.rem(a + k, chans)], parts.at[k - 1], s1, k - 1, rows[k - 1]) for k in range(1, chans)]
    total = part[a].astype(jnp.float32)
    for k in range(chans - 1):
        copies[k].wait_recv()
        total = total + parts[k].astype(jnp.float32)
    gath[b] = total.astype(jnp.bfloat16)
    spread(lambda i: gath.at[i], None, chips, chip, core, far, mate, s2, s3)
    first = jnp.zeros((size, 1), jnp.float32)
    second = jnp.zeros((size, 1), jnp.float32)
    for i in range(hids):
        x = gath[i].astype(jnp.float32)
        first = first + jnp.sum(x, axis=1, keepdims=True)
        second = second + jnp.sum(x * x, axis=1, keepdims=True)
    mean = first / (width * hids)
    scale = lax.rsqrt(second / (width * hids) - mean * mean + epsilon)
    stat[...] = jnp.where(lax.broadcasted_iota(jnp.int32, stat.shape, 1) == 0, mean, scale)
    ratio = hids // chans
    moved = []
    for k in range(1, chans):
        to = lax.rem(a + k, chans)
        moved.append(send(stat, stats.at[a], s5, k - 1, rows[k - 1]))
        moved.append(send(gath.at[pl.ds(to * ratio, ratio)], whole.at[a], s4, k - 1, rows[k - 1]))
    for copy in copies:
        copy.wait_send()

    def emit(i, x_of, st):
        for r in range(ratio):
            cs = slice(r * width, (r + 1) * width)
            x = x_of(r)
            own_ref[i, :, cs] = x
            normed_ref[i, :, cs] = (
                (x.astype(jnp.float32) - st[:, 0:1]) * st[:, 1:2] * gain[:, cs]
            ).astype(jnp.bfloat16)

    emit(a, lambda r: gath[a * ratio + r], stat[...])
    for copy in moved:
        copy.wait()
    for k in range(1, chans):
        i = lax.rem(a + k, chans)
        emit(i, lambda r: whole[i, r], stats[i])


def layer_rows(partial, gain, chans, hids):
    tok, width = partial.shape
    size = tok // chans
    wide = gain.shape[0]
    vm = pl.BlockSpec(memory_space=pltpu.VMEM)
    dma = pltpu.SemaphoreType.DMA
    shape = jax.ShapeDtypeStruct((chans, size, wide), jnp.bfloat16)
    normed, own = pl.pallas_call(
        functools.partial(layer_kernel, chans, hids), out_shape=(shape, shape), in_specs=[vm, vm], out_specs=(vm, vm),
        scratch_shapes=[
            pltpu.VMEM((chans - 1, size, width), jnp.bfloat16), pltpu.VMEM((hids, size, width), jnp.bfloat16),
            pltpu.VMEM((size, HS), jnp.float32), pltpu.VMEM((chans, hids // chans, size, width), jnp.bfloat16),
            pltpu.VMEM((chans, size, HS), jnp.float32),
            dma((2, chans - 1)), dma((2, hids // 2 - 1)), dma((2, hids // 2)), dma((2, chans - 1)), dma((2, chans - 1))],
        compiler_params=pltpu.CompilerParams(collective_id=1, has_side_effects=True, vmem_limit_bytes=40 << 20),
        name="layer_rows",
    )(partial.reshape(chans, size, width), gain.reshape(1, wide))
    return normed.reshape(tok, wide), own.reshape(tok, wide)


def finish_kernel(chans, hids, heads, qkv, up, bias, qkv_out, hid_out, qkv_in, up_in, s1, s2, s3, s4):
    a, rows = lax.axis_index("chan"), [{"chan": lax.rem(lax.axis_index("chan") + k, chans)} for k in range(1, chans)]
    greet(rows)
    got_q = [send(qkv.at[:, lax.rem(a + k, chans)], qkv_in.at[k - 1], s1, k - 1, rows[k - 1]) for k in range(1, chans)]
    got_u = [send(up.at[lax.rem(a + k, chans)], up_in.at[k - 1], s2, k - 1, rows[k - 1]) for k in range(1, chans)]
    for copy in got_q:
        copy.wait_recv()
    for h in range(3 * heads):
        kind, hs = h // heads, slice(h % heads * HS, (h % heads + 1) * HS)
        x = qkv[kind, a, :, hs].astype(jnp.float32)
        for k in range(chans - 1):
            x = x + qkv_in[k, kind, :, hs].astype(jnp.float32)
        if h < 2 * heads:
            x = x * lax.rsqrt(jnp.mean(x * x, axis=-1, keepdims=True) + epsilon)
        qkv_out[h, a] = x.astype(jnp.bfloat16)
    put_q = [send(qkv_out.at[:, a], qkv_out.at[:, a], s3, k, peer) for k, peer in enumerate(rows)]
    for copy in got_u:
        copy.wait_recv()
    step = HS
    for n in range(up.shape[2] // step):
        cs = slice(n * step, (n + 1) * step)
        x = up[a, :, cs].astype(jnp.float32)
        for k in range(chans - 1):
            x = x + up_in[k, :, cs].astype(jnp.float32)
        x = x + bias[:, cs]
        hid_out[a, :, cs] = ((0.5 * x) * (1.0 + lax.erf(x * math.sqrt(0.5)))).astype(jnp.bfloat16)
    put_u = [send(hid_out.at[a], hid_out.at[a], s4, k, peer) for k, peer in enumerate(rows)]
    for copy in got_q + got_u:
        copy.wait_send()
    for copy in put_q + put_u:
        copy.wait()


def finish(qkv, up, bias, heads, chans, hids):
    tok, wide = qkv.shape[1:]
    size, units = tok // chans, up.shape[1]
    vm = pl.BlockSpec(memory_space=pltpu.VMEM)
    dma = pltpu.SemaphoreType.DMA
    q, u = pl.pallas_call(
        functools.partial(finish_kernel, chans, hids, heads),
        out_shape=(jax.ShapeDtypeStruct((3 * heads, chans, size, HS), jnp.bfloat16), jax.ShapeDtypeStruct((chans, size, units), jnp.bfloat16)),
        in_specs=[vm] * 3, out_specs=(vm, vm),
        scratch_shapes=[
            pltpu.VMEM((chans - 1, 3, size, wide), jnp.bfloat16), pltpu.VMEM((chans - 1, size, units), jnp.bfloat16)]
        + [dma((2, chans - 1))] * 4,
        compiler_params=pltpu.CompilerParams(collective_id=2, has_side_effects=True, vmem_limit_bytes=40 << 20),
        name="finish",
    )(qkv.reshape(3, chans, size, wide), up.reshape(chans, size, units), bias.reshape(1, units))
    return q.reshape(3, heads, tok, HS), u.reshape(tok, units)


def total_kernel(hids, term, own, out, pair, half, pieces, s1, s2, s3, s4):
    b = lax.axis_index("hid")
    chips, chip, core = hids // 2, b // 2, b % 2
    far = [{"hid": lax.rem(chip + k, chips) * 2 + core} for k in range(1, chips)]
    mate = {"hid": chip * 2 + (1 - core)}
    greet(far + [mate])
    across = send(term.at[1 - core], pair, s1, 0, mate)
    across.wait_recv()
    for i in range(chips):
        half[i] = (term[core, i].astype(jnp.float32) + pair[i].astype(jnp.float32)).astype(jnp.bfloat16)
    copies = [send(half.at[lax.rem(chip + k, chips)], pieces.at[k - 1], s2, k - 1, far[k - 1]) for k in range(1, chips)]
    value = half[chip].astype(jnp.float32)
    for k in range(chips - 1):
        copies[k].wait_recv()
        value = value + pieces[k].astype(jnp.float32)
    out[core, chip] = (value + own[core, chip].astype(jnp.float32)).astype(jnp.bfloat16)
    spread(lambda i: out.at[i % 2, i // 2], None, chips, chip, core, far, mate, s3, s4)
    across.wait_send()
    for copy in copies:
        copy.wait_send()


def total(term, own, hids):
    tok, wide = term.shape
    chips, size = hids // 2, tok // hids
    vm = pl.BlockSpec(memory_space=pltpu.VMEM)
    dma = pltpu.SemaphoreType.DMA
    out = pl.pallas_call(
        functools.partial(total_kernel, hids),
        out_shape=jax.ShapeDtypeStruct((2, chips, size, wide), jnp.bfloat16), in_specs=[vm] * 2, out_specs=vm,
        scratch_shapes=[
            pltpu.VMEM((chips, size, wide), jnp.bfloat16), pltpu.VMEM((chips, size, wide), jnp.bfloat16),
            pltpu.VMEM((chips - 1, size, wide), jnp.bfloat16),
            dma((2, 1)), dma((2, chips - 1)), dma((2, chips - 1)), dma((2, chips))],
        compiler_params=pltpu.CompilerParams(collective_id=3, has_side_effects=True, vmem_limit_bytes=40 << 20),
        name="total",
    )(term.reshape(2, chips, size, wide), own.reshape(2, chips, size, wide))
    return out.reshape(tok, wide)


def on_device(
    chans,
    hids,
    pixels,
    patch_weight,
    channel_embed,
    pool_query,
    group_mix,
    assign,
    ln_gain,
    w_qkv,
    w_up,
    b_up,
    w_out,
    w_down,
):
    tok_count = pixels.shape[1]
    width_hid = patch_weight.shape[2]
    heads_dev = width_hid // HS
    partial_value = pool(pixels, patch_weight, channel_embed, pool_query, group_mix, assign)
    normed_input, own_cols = layer_rows(partial_value, ln_gain, chans, hids)
    qkv_part = jnp.einsum("td,dke->kte", normed_input, w_qkv, preferred_element_type=jnp.float32)
    up_part = jnp.dot(normed_input, w_up, preferred_element_type=jnp.float32)
    qkv_rows, hidden = finish(
        qkv_part.astype(jnp.bfloat16), up_part.astype(jnp.bfloat16), b_up, heads_dev, chans, hids
    )
    images = tok_count // PATCHES
    queries, keys, values = qkv_rows.reshape(3, heads_dev, images, PATCHES, HS)
    scores = jnp.einsum("hbqe,hbke->hbqk", queries, keys, preferred_element_type=jnp.float32) * (
        2.0 / math.sqrt(HS)
    )
    expo = jnp.exp(scores)
    probs = (expo / jnp.sum(expo, axis=-1, keepdims=True)).astype(jnp.bfloat16)
    attended = jnp.einsum("hbqk,hbke->bqhe", probs, values, preferred_element_type=jnp.float32)
    attended = attended.astype(jnp.bfloat16).reshape(tok_count, width_hid)
    term = jnp.dot(attended, w_out, preferred_element_type=jnp.float32) + jnp.dot(
        hidden, w_down, preferred_element_type=jnp.float32
    )
    term = term.astype(jnp.bfloat16)
    if tok_count % (16 * hids) == 0:
        return total(term, own_cols, hids)
    mixed = lax.psum(term, "hid").astype(jnp.float32)
    return (own_cols.astype(jnp.float32) + mixed).astype(jnp.bfloat16)


def solution(mesh):
    in_specs = (
        P("chan", None, None),
        P("chan", None, "hid"),
        P("chan", "hid"),
        P("chan", "hid"),
        P("chan", "hid"),
        P("chan"),
        P("chan"),
        P("chan", None, "hid"),
        P("chan", "hid"),
        P("hid"),
        P("hid", "chan"),
        P("hid", "chan"),
    )
    out_specs = P(None, "chan")
    chans, hids = mesh.shape["chan"], mesh.shape["hid"]
    return jax.shard_map(
        functools.partial(on_device, chans, hids), mesh=mesh, in_specs=in_specs, out_specs=out_specs, check_vma=False
    )
```
